32 devices in a mesh: seq: 4 (over y, x), span: 4 (over z), kvg: 2 (over core).
Axes of the slice: x: 2, y: 2, z: 4, core: 2. Of those that a mesh axis runs over, the one named last changes fastest.
Arguments:
- query_rows: bfloat16 [8704, 1792], P(('seq', 'span'), 'kvg'), parts along dimension 0, may hold values from -256 to 256
- key_rows: bfloat16 [8704, 256], P(('seq', 'span'), 'kvg'), parts along dimension 0, may hold values from -6 to 6
- value_rows: bfloat16 [8704, 256], P(('seq', 'span'), 'kvg'), parts along dimension 0, may hold values from -6 to 6
- out_grad: bfloat16 [8704, 1792], P(('seq', 'span'), 'kvg'), parts along dimension 0, may hold values from -6 to 6
- ratios: int32 [16], P('seq'), parts along dimension 0, may hold values from 16 to 64, as said below
Outputs:
- attended: bfloat16 [8704, 1792], P(('seq', 'span'), 'kvg'), parts along dimension 0
- query_grad: bfloat16 [8704, 1792], P(('seq', 'span'), 'kvg'), parts along dimension 0
- key_grad: bfloat16 [8704, 256], P(('seq', 'span'), 'kvg'), parts along dimension 0
- value_grad: bfloat16 [8704, 256], P(('seq', 'span'), 'kvg'), parts along dimension 0
The draws below stay inside these ranges and needn't reach their ends.
There are 4 independent parts, one for each index of `seq`. The reference program is written for one: setup_inputs(seed, part) draws one part's arguments, and reference() takes and returns one part's arrays. A program takes and returns all parts, laid end to end along the dimension named above; each array names one. Nothing has to cross between parts.
Inputs may be any that keep to these rules, and one draw needn't show every extreme that they name: `ratios`: every ratio is 16, 32 or 64, and some span of every sequence has 16.
All inputs are finite; a program needn't handle non-finite values.
Results may differ from the reference program's by a relative error of at most 0.0096.
Values may be sent and summed in bfloat16 or wider, within the bound.
A program may use at most 64 MiB of HBM per device.

```python
import jax
import jax.numpy as jnp
from jax import lax

SPAN = 512
RMIN = 16
HD = 128
QPG = 7
GROUPS = 2
BMAX = 32
SEG = 544
NCH = 4
ROWS = 2176
NB = 128


def pair_draw(key):
    base_query = 2.0 * jax.random.normal(jax.random.fold_in(key, 101), (ROWS, GROUPS * QPG * HD), jnp.float32)
    query_draw = jnp.clip(base_query, -12.0, 12.0)
    key_draw = jnp.clip(jax.random.normal(jax.random.fold_in(key, 202), (ROWS, GROUPS * HD), jnp.float32), -6.0, 6.0)
    return (query_draw, key_draw)


def draw_query_rows(key, part):
    return pair_draw(key)[0].astype(jnp.bfloat16)


def draw_key_rows(key, part):
    return pair_draw(key)[1].astype(jnp.bfloat16)


def draw_ratios(key, part):
    powers = jax.random.randint(jax.random.fold_in(key, 404), (NCH,), 0, 3, dtype=jnp.int32)
    chosen = jax.random.randint(jax.random.fold_in(key, 505), (), 0, NCH, dtype=jnp.int32)
    powers = jnp.where(jnp.arange(NCH, dtype=jnp.int32) == chosen, 0, powers)
    return jnp.where(powers == 0, RMIN, jnp.where(powers == 1, 2 * RMIN, 4 * RMIN)).astype(jnp.int32)


def steps_of(rng, dims, cuts, least, top_value):
    gain, own = 1.0, jax.random.fold_in(rng, 6)
    for dim, shards_of in cuts:
        steps = jnp.exp(jax.random.uniform(jax.random.fold_in(own, dim), (shards_of,), jnp.float32, least / len(cuts), top_value / len(cuts)))
        gain = gain * jnp.repeat(steps, dims[dim] // shards_of).reshape([-1 if axis == dim else 1 for axis in range(len(dims))])
    return gain


def gaussian(key, extent, deviation, limit, split=(), held_as=jnp.bfloat16):
    values = deviation * jax.random.normal(key, extent, jnp.float32)
    if split:
        values = values * steps_of(key, extent, split, -0.22, 0.18)
    return jnp.clip(values, -limit, limit).astype(held_as)


def setup_inputs(seed: int = 0, part: int = 0) -> dict:
    streams_of = jax.random.split(jax.random.key(seed), 6)
    part_splits = jax.random.split(jax.random.fold_in(streams_of[5], part), 6)
    query_rows = draw_query_rows(jax.random.fold_in(jax.random.fold_in(streams_of[5], part), 71), part)
    key_rows = draw_key_rows(jax.random.fold_in(jax.random.fold_in(streams_of[5], part), 71), part)
    value_rows = gaussian(part_splits[2], (ROWS, GROUPS * HD), 1.0, 6.0, ((0, 4), (1, 2)))
    out_grad = gaussian(part_splits[3], (ROWS, GROUPS * QPG * HD), 1.0, 6.0, ((0, 4), (1, 2)))
    ratios = draw_ratios(jax.random.fold_in(jax.random.fold_in(streams_of[5], part), 71), part)
    return {"query_rows": query_rows, "key_rows": key_rows, "value_rows": value_rows, "out_grad": out_grad, "ratios": ratios}


floor_score = -1.0e30


def product(pattern, first_arg, second_arg):
    return jnp.einsum(pattern, first_arg.astype(jnp.float32), second_arg.astype(jnp.float32))


def build_masks(ratios, first_span, local_spans):
    counts = SPAN // ratios
    slot_ids = jnp.arange(BMAX, dtype=jnp.int32)
    live_slots = (slot_ids[None, :] < counts[:, None]).reshape(-1)
    span_ids = first_span + jnp.arange(local_spans, dtype=jnp.int32)
    owner_span = jnp.arange(live_slots.shape[0], dtype=jnp.int32) // BMAX
    beacon_mask = (owner_span[None, :] < span_ids[:, None]) & live_slots[None, :]
    local_ratio = lax.dynamic_slice_in_dim(ratios, first_span, local_spans)
    local_count = SPAN // local_ratio
    positions = jnp.arange(SEG, dtype=jnp.int32)
    is_beacon = positions >= SPAN
    slot_of = positions - SPAN
    key_order = jnp.where(is_beacon[None, :], (slot_of[None, :] + 1) * local_ratio[:, None] - 1, positions[None, :])
    live_row = jnp.logical_not(is_beacon[None, :]) | (slot_of[None, :] < local_count[:, None])
    raw_key = jnp.logical_not(is_beacon)[None, None, :] & (key_order[:, None, :] <= key_order[:, :, None])
    beacon_key = is_beacon[None, :, None] & is_beacon[None, None, :] & live_row[:, None, :] & (positions[None, None, :] <= positions[None, :, None])
    return beacon_mask, raw_key | beacon_key, live_row.astype(jnp.float32)


def attend_head(query_head, grad_head, beacon_keys, beacon_values, own_keys, own_values, beacon_mask, own_mask, live_rows):
    score_scale = HD ** -0.5
    beacon_scores = jnp.where(beacon_mask[:, None, :], product("csd,bd->csb", query_head, beacon_keys) * score_scale, floor_score)
    own_scores = jnp.where(own_mask, product("csd,ctd->cst", query_head, own_keys) * score_scale, floor_score)
    row_top = jnp.maximum(jnp.max(beacon_scores, -1), jnp.max(own_scores, -1))
    row_total = jnp.sum(jnp.exp(beacon_scores - row_top[..., None]), -1) + jnp.sum(jnp.exp(own_scores - row_top[..., None]), -1)
    row_lse = row_top + jnp.log(row_total)
    beacon_probs = jnp.exp(beacon_scores - row_lse[..., None])
    own_probs = jnp.exp(own_scores - row_lse[..., None])
    beacon_weights = beacon_probs.astype(jnp.bfloat16)
    own_weights = own_probs.astype(jnp.bfloat16)
    mixed_rows = product("csb,bd->csd", beacon_weights, beacon_values) + product("cst,ctd->csd", own_weights, own_values)
    attended = (mixed_rows * live_rows[..., None]).astype(jnp.bfloat16)
    grad_rows = grad_head * live_rows.astype(jnp.bfloat16)[..., None]
    row_delta = jnp.sum(grad_rows.astype(jnp.float32) * attended.astype(jnp.float32), -1)
    beacon_sgrad = (beacon_probs * (product("csd,bd->csb", grad_rows, beacon_values) - row_delta[..., None])).astype(jnp.bfloat16)
    own_sgrad = (own_probs * (product("csd,ctd->cst", grad_rows, own_values) - row_delta[..., None])).astype(jnp.bfloat16)
    query_grad = (score_scale * (product("csb,bd->csd", beacon_sgrad, beacon_keys) + product("cst,ctd->csd", own_sgrad, own_keys))).astype(jnp.bfloat16)
    beacon_kgrad = score_scale * product("csb,csd->bd", beacon_sgrad, query_head)
    beacon_vgrad = product("csb,csd->bd", beacon_weights, grad_rows)
    own_kgrad = score_scale * product("cst,csd->ctd", own_sgrad, query_head)
    own_vgrad = product("cst,csd->ctd", own_weights, grad_rows)
    return attended, query_grad, beacon_kgrad, beacon_vgrad, own_kgrad, own_vgrad


def reference(query_rows, key_rows, value_rows, out_grad, ratios):
    beacon_mask, own_mask, live_rows = build_masks(ratios, 0, NCH)
    query_blocks = query_rows.reshape(NCH, SEG, GROUPS, QPG, HD)
    grad_blocks = out_grad.reshape(NCH, SEG, GROUPS, QPG, HD)
    key_blocks = key_rows.reshape(NCH, SEG, GROUPS, HD)
    value_blocks = value_rows.reshape(NCH, SEG, GROUPS, HD)
    attended_parts, query_parts, key_parts, value_parts = [], [], [], []
    for group_index in range(GROUPS):
        own_keys = key_blocks[:, :, group_index]
        own_values = value_blocks[:, :, group_index]
        beacon_keys = own_keys[:, SPAN:].reshape(NB, HD)
        beacon_values = own_values[:, SPAN:].reshape(NB, HD)
        beacon_ksum = jnp.zeros((NB, HD), jnp.float32)
        beacon_vsum = jnp.zeros((NB, HD), jnp.float32)
        own_ksum = jnp.zeros((NCH, SEG, HD), jnp.float32)
        own_vsum = jnp.zeros((NCH, SEG, HD), jnp.float32)
        head_outputs, head_grads = [], []
        for head_index in range(QPG):
            result = attend_head(query_blocks[:, :, group_index, head_index], grad_blocks[:, :, group_index, head_index], beacon_keys, beacon_values, own_keys, own_values, beacon_mask, own_mask, live_rows)
            head_outputs.append(result[0])
            head_grads.append(result[1])
            beacon_ksum = beacon_ksum + result[2]
            beacon_vsum = beacon_vsum + result[3]
            own_ksum = own_ksum + result[4]
            own_vsum = own_vsum + result[5]
        attended_parts.append(jnp.stack(head_outputs, 2))
        query_parts.append(jnp.stack(head_grads, 2))
        key_total = jnp.concatenate([own_ksum[:, :SPAN], own_ksum[:, SPAN:] + beacon_ksum.reshape(NCH, BMAX, HD)], 1)
        value_total = jnp.concatenate([own_vsum[:, :SPAN], own_vsum[:, SPAN:] + beacon_vsum.reshape(NCH, BMAX, HD)], 1)
        key_parts.append(key_total.astype(jnp.bfloat16))
        value_parts.append(value_total.astype(jnp.bfloat16))
    attended = jnp.stack(attended_parts, 2).reshape(ROWS, GROUPS * QPG * HD)
    query_grad = jnp.stack(query_parts, 2).reshape(ROWS, GROUPS * QPG * HD)
    key_grad = jnp.stack(key_parts, 2).reshape(ROWS, GROUPS * HD)
    value_grad = jnp.stack(value_parts, 2).reshape(ROWS, GROUPS * HD)
    return attended, query_grad, key_grad, value_grad
```

```python
import functools
import math

import jax
import jax.numpy as jnp
from jax import lax
from jax.experimental import pallas as pl
from jax.experimental.pallas import tpu as pltpu
from jax.sharding import PartitionSpec as P

SPAN = 512
HD = 128
BMAX = 32
BLK = 256
SUB = 128

SCALE = HD ** (-0.5)
SCALE_LOG2E = SCALE * math.log2(math.e)
FLOOR = -1e30

f32 = jnp.float32
bf16 = jnp.bfloat16


def nt(a, b):
    return lax.dot_general(a, b, (((1,), (1,)), ((), ())), preferred_element_type=f32)


def nn(a, b):
    return lax.dot_general(a, b, (((1,), (0,)), ((), ())), preferred_element_type=f32)


def interleave(blocks):
    waiting, active = list(blocks), []
    while waiting or active:
        if waiting:
            active.append(waiting.pop(0))
        active = [block for block in active if next(block, "end") != "end"]


def fold(op, x, rows=32):
    out = x[0:rows]
    for i in range(rows, x.shape[0], rows):
        out = op(out, x[i : i + rows])
    return out


def plan(heads):
    blocks = []
    for t in range(SPAN // SUB):
        for h in range(0, heads - 1, 2):
            blocks.append((h, 2, t * SUB, SUB, (t + 1) * SUB))
        if heads % 2 and t % 2:
            blocks.append((heads - 1, 1, (t - 1) * SUB, BLK, (t + 1) * SUB))
    return blocks


def kernel(
    n, heads,
    ratios_hbm, q_hbm, k_hbm, v_hbm, g_hbm,
    o_s, dq_s, dk_out, dv_out,
    q_s, g_s, k_s, v_s, kt_s, vt_s, kv_s, kbt_s, vbt_s,
    s_s, sl_s, e_s, sg_s, pb_s, sb_s, qt_s, gt_s, stat_s, bias_s, bbias_s, pair_s, single_s,
    term_s, send_s, recv_s, dk_s, dv_s,
    ratios_ref, ratio_sem, in_sem, q_sem, g_sem, kv_send, kv_recv, term_send, term_recv,
):
    me = lax.axis_index("span")
    nb = n * BMAX
    seen = (n - 1) * BMAX
    bands = SPAN // SUB
    blocks = plan(heads)
    last = len(blocks)
    mine = pl.ds(pl.multiple_of(me * BMAX, BMAX), BMAX)
    left, right = pl.ds(0, HD), pl.ds(HD, HD)

    ratio_copy = pltpu.make_async_copy(ratios_hbm, ratios_ref, ratio_sem)
    k_copy = pltpu.make_async_copy(k_hbm.at[pl.ds(0, SPAN)], k_s, in_sem.at[0])
    v_copy = pltpu.make_async_copy(v_hbm.at[pl.ds(0, SPAN)], v_s, in_sem.at[1])
    kb_copy = pltpu.make_async_copy(
        k_hbm.at[pl.ds(SPAN, BMAX)], kv_s.at[mine, left], in_sem.at[2]
    )
    vb_copy = pltpu.make_async_copy(
        v_hbm.at[pl.ds(SPAN, BMAX)], kv_s.at[mine, right], in_sem.at[3]
    )

    def band_copy(src, dst, sem, t):
        rows = pl.ds(t * SUB, SUB if t < bands else BMAX)
        return pltpu.make_async_copy(src.at[rows], dst.at[rows], sem.at[t])

    kv_s[...] = jnp.zeros_like(kv_s)
    barrier = pltpu.get_barrier_semaphore()
    for step in range(1, n):
        @pl.when(me >= step)
        def _():
            pl.semaphore_signal(
                barrier, inc=1, device_id={"span": me - step},
                device_id_type=pl.DeviceIdType.MESH,
            )

    k_copy.start()
    band_copy(q_hbm, q_s, q_sem, 0).start()
    v_copy.start()
    band_copy(g_hbm, g_s, g_sem, 0).start()
    ratio_copy.start()

    recv_s[...] = jnp.zeros_like(recv_s)

    kb_copy.start()
    vb_copy.start()
    for t in range(1, bands + 1):
        band_copy(q_hbm, q_s, q_sem, t).start()
        band_copy(g_hbm, g_s, g_sem, t).start()

    term_s[...] = jnp.zeros_like(term_s)
    dk_s[...] = jnp.zeros_like(dk_s)
    dv_s[...] = jnp.zeros_like(dv_s)
    for b in range(last):
        for ref in (pb_s, sb_s):
            ref[b, pl.ds(seen, BMAX), :] = jnp.zeros((BMAX, BLK), bf16)
    row = lax.broadcasted_iota(jnp.int32, (BLK, BLK), 0)
    col = lax.broadcasted_iota(jnp.int32, (BLK, BLK), 1)
    single_s[...] = jnp.where(row <= col, 0.0, FLOOR)
    pair_s[...] = jnp.where(row <= lax.rem(col, SUB), 0.0, FLOOR)[0:SUB]

    ratio_copy.wait()
    own_ratio = ratios_ref[me]
    key_id = lax.broadcasted_iota(jnp.int32, (nb, BLK), 0)
    lane_slot = lax.rem(lax.broadcasted_iota(jnp.int32, (nb, BLK), 1), BMAX)
    key_slot = lax.rem(key_id, BMAX)
    key_span = key_id // BMAX
    key_ratio = jnp.zeros((nb, BLK), jnp.int32)
    for s in range(n):
        key_ratio = jnp.where(key_span == s, ratios_ref[s], key_ratio)
    live = (key_slot + 1) * key_ratio <= SPAN
    before = live & (key_span < me)
    bias_s[...] = jnp.where(before, 0.0, FLOOR)
    bbias_s[...] = jnp.where(
        before | (live & (key_span == me) & (key_slot <= lane_slot)), 0.0, FLOOR
    )
    reach = (lax.rem(lax.broadcasted_iota(jnp.int32, (SUB, BLK), 1), BMAX) + 1) * own_ratio
    sub_row = lax.broadcasted_iota(jnp.int32, (SUB, BLK), 0)
    row_live = (lax.broadcasted_iota(jnp.int32, (BMAX, HD), 0) + 1) * own_ratio <= SPAN
    lane_live = (
        lax.rem(lax.broadcasted_iota(jnp.int32, (1, BLK), 1), BMAX) + 1
    ) * own_ratio <= SPAN

    def kv_copy(step):
        return pltpu.make_async_remote_copy(
            src_ref=kv_s.at[mine], dst_ref=kv_s.at[mine],
            send_sem=kv_send.at[step - 1], recv_sem=kv_recv.at[step - 1],
            device_id={"span": lax.rem(me + step, n)}, device_id_type=pl.DeviceIdType.MESH,
        )

    def send_kv(first, part):
        @pl.when(me == 0 if first else (me > 0) & (me < n - 1))
        def _():
            if part == 0:
                pl.semaphore_wait(barrier, n - 1 - me)
            for step in range(n - 1, 0, -1):
                @pl.when(me + step == n - 1 if part == 0 else me + step < n - 1)
                def _():
                    kv_copy(step).start()

    def wait_kv(first):
        for step in range(1, n):
            @pl.when(me == step if first else me > step)
            def _():
                kv_copy(step).wait_recv()

    def call(*functions):
        for function in functions:
            function()
        yield

    def load(ref, b):
        if b == last:
            tail = pl.ds(SPAN, BMAX)
            parts = [ref[tail, pl.ds(h * HD, HD)] for h in range(heads)]
            parts.append(jnp.zeros((BLK - heads * BMAX, HD), bf16))
        else:
            h, count, start, size, _ = blocks[b]
            parts = [
                ref[pl.ds(start, size), pl.ds((h + i) * HD, HD)] for i in range(count)
            ]
        return jnp.concatenate(parts, 0)

    def scatter(ref, b, value):
        if b == last:
            for h in range(heads):
                ref[pl.ds(SPAN, BMAX), pl.ds(h * HD, HD)] = value[h * BMAX : (h + 1) * BMAX]
        else:
            h, count, start, size, _ = blocks[b]
            for i in range(count):
                ref[pl.ds(start, size), pl.ds((h + i) * HD, HD)] = value[
                    i * size : (i + 1) * size
                ]

    def keys_of(b):
        return SPAN if b == last else blocks[b][4]

    def own_scores(b, wait):
        wait()
        if b == last:
            for h in range(heads):
                spot = (pl.ds(SPAN, BMAX), pl.ds(h * HD, HD))
                g_s[spot] = jnp.where(row_live, g_s[spot].astype(f32), 0.0).astype(bf16)
        keys = keys_of(b)
        scores = nt(k_s[pl.ds(0, keys), :], load(q_s, b))
        top = None
        for c in range(0, keys, SUB):
            part = scores[c : c + SUB]
            if b == last:
                part = jnp.where(sub_row + c < reach, part, FLOOR)
            elif blocks[b][1] == 2 and c == keys - SUB:
                part = part + pair_s[...]
            elif blocks[b][1] == 1 and c >= keys - BLK:
                at = c - (keys - BLK)
                part = part + single_s[at : at + SUB, :]
            s_s[b, pl.ds(c, SUB), :] = part
            part = fold(jnp.maximum, part)
            top = part if top is None else jnp.maximum(top, part)
        qt_s[b] = load(q_s, b).T
        yield
        slope = nt(v_s[pl.ds(0, keys), :], load(g_s, b))
        gt_s[b] = load(g_s, b).T
        sl_s[b, pl.ds(0, keys), :] = slope
        top = jnp.max(top, axis=0, keepdims=True)
        stat_s[b, 0:1, :] = top
        yield
        total = dot = None
        for c in range(0, keys, SUB):
            e = jnp.exp2((s_s[b, pl.ds(c, SUB), :] - top) * SCALE_LOG2E)
            e_s[b, pl.ds(c, SUB), :] = e.astype(bf16)
            part = fold(jnp.add, e)
            total = part if total is None else total + part
            part = fold(jnp.add, e * sl_s[b, pl.ds(c, SUB), :])
            dot = part if dot is None else dot + part
        stat_s[b, 1:2, :] = jnp.sum(total, axis=0, keepdims=True)
        stat_s[b, 2:3, :] = jnp.sum(dot, axis=0, keepdims=True)

    def band_waits(t):
        def run():
            band_copy(q_hbm, q_s, q_sem, t).wait()
            band_copy(g_hbm, g_s, g_sem, t).wait()
        return run

    waits, t = [], 0
    for h, count, start, size, _ in blocks:
        need = (start + size) // SUB - 1
        waits.append(band_waits(need) if need >= t else lambda: None)
        t = max(t, need + 1)
    waits.append(band_waits(bands))

    k_copy.wait()
    v_copy.wait()

    def beacon_early(b):
        count = nb if b == last else seen
        used = pl.ds(BMAX, count - BMAX)
        bias = bbias_s if b == last else bias_s
        scores = nn(kv_s[used, left], qt_s[b]) + bias[used, :]
        slope = nn(kv_s[used, right], gt_s[b])
        top = fold(jnp.maximum, scores)
        yield
        own_top = stat_s[b, 0:1, :]
        top = jnp.maximum(own_top, jnp.max(top, axis=0, keepdims=True))
        e = jnp.exp2((scores - top) * SCALE_LOG2E)
        shrink = jnp.exp2((own_top - top) * SCALE_LOG2E)
        pb_s[b, used, :] = e.astype(bf16)
        total = jnp.sum(fold(jnp.add, e), axis=0, keepdims=True)
        dot = jnp.sum(fold(jnp.add, e * slope), axis=0, keepdims=True)
        stat_s[b, 0:1, :] = top
        stat_s[b, 1:2, :] = shrink * stat_s[b, 1:2, :] + total
        stat_s[b, 2:3, :] = shrink * stat_s[b, 2:3, :] + dot
        stat_s[b, 3:4, :] = shrink

    def beacon_late(b):
        late = pl.ds(0, BMAX)
        bias = bbias_s if b == last else bias_s
        scores = nn(kv_s[late, left], qt_s[b]) + bias[late, :]
        slope = nn(kv_s[late, right], gt_s[b])
        yield
        old_top = stat_s[b, 0:1, :]
        top = jnp.maximum(old_top, jnp.max(scores, axis=0, keepdims=True))
        e = jnp.exp2((scores - top) * SCALE_LOG2E)
        shrink = jnp.exp2((old_top - top) * SCALE_LOG2E)
        total = shrink * stat_s[b, 1:2, :] + jnp.sum(e, axis=0, keepdims=True)
        dot = shrink * stat_s[b, 2:3, :] + jnp.sum(e * slope, axis=0, keepdims=True)
        inverse = 1.0 / total
        shrink = shrink * inverse
        delta = inverse * dot
        if b == last:
            delta = jnp.where(lane_live, delta, 0.0)
        stat_s[b, 3:4, :] = shrink * stat_s[b, 3:4, :]
        stat_s[b, 4:5, :] = delta
        stat_s[b, 5:6, :] = shrink
        yield
        probs = e * inverse
        pb_s[b, late, :] = probs.astype(bf16)
        sb_s[b, late, :] = (probs * (slope - delta)).astype(bf16)

    def beacon_rest(b):
        used = pl.ds(BMAX, (nb if b == last else seen) - BMAX)
        slope = nn(kv_s[used, right], gt_s[b])
        probs = pb_s[b, used, :].astype(f32) * stat_s[b, 5:6, :]
        pb_s[b, used, :] = probs.astype(bf16)
        yield
        sb_s[b, used, :] = (probs * (slope - stat_s[b, 4:5, :])).astype(bf16)

    def term_part(members, used):
        for ref, rows, cols in ((pb_s, g_s, right), (sb_s, q_s, left)):
            term_s[used, cols] += nn(
                jnp.concatenate([ref[b, used, :] for b in members], 1),
                jnp.concatenate([load(rows, b) for b in members], 0),
            )
            yield

    def with_terms(part, size, used_of):
        order, ready = [], None
        for at in range(0, last + 1, size):
            members = list(range(at, min(at + size, last + 1)))
            order += [part(b) for b in members]
            if ready:
                order.append(term_part(ready, used_of(ready)))
            ready = members
        return order + [call(), term_part(ready, used_of(ready))]

    order = [own_scores(b, waits[b]) for b in range(last + 1)]
    order.insert(14 + 1, call(lambda: send_kv(True, 1)))
    order.insert(14, call(lambda: send_kv(True, 0)))
    order.insert(3 + 1, call(lambda: send_kv(False, 1)))
    order.insert(3, call(kb_copy.wait, vb_copy.wait, lambda: send_kv(False, 0)))
    order.append(call(lambda: wait_kv(False)))
    order += [beacon_early(b) for b in range(last + 1)]
    order.append(call(lambda: wait_kv(True)))
    interleave(order + with_terms(beacon_late, 4, lambda members: pl.ds(0, BMAX)))

    def term_copy(step):
        peer = lax.rem(me + (n - step), n)
        return pltpu.make_async_remote_copy(
            src_ref=send_s.at[pl.ds(pl.multiple_of(peer * BMAX, BMAX), BMAX)],
            dst_ref=recv_s.at[step - 1],
            send_sem=term_send.at[step - 1], recv_sem=term_recv.at[step - 1],
            device_id={"span": peer}, device_id_type=pl.DeviceIdType.MESH,
        )

    def send_terms(first):
        rows = pl.ds(0, BMAX) if first else pl.ds(BMAX, nb - BMAX)
        send_s[rows, :] = term_s[rows, :].astype(bf16)
        for step in range(n - 1, 0, -1):
            @pl.when(me == step if first else me > step)
            def _():
                term_copy(step).start()

    send_terms(True)
    kt_s[...] = k_s[...].T
    vt_s[...] = v_s[...].T
    kbt_s[...] = kv_s[:, left].T
    vbt_s[...] = kv_s[:, right].T

    def own_part(b):
        keys = keys_of(b)
        delta = stat_s[b, 4:5, :]
        half = stat_s[b, 3:4, :].astype(bf16)
        for c in range(0, keys, SUB):
            spot = pl.ds(c, SUB)
            probs = e_s[b, spot, :] * half
            e_s[b, spot, :] = probs
            sg_s[b, spot, :] = (sl_s[b, spot, :] - delta).astype(bf16) * probs
        yield
        out = nn(
            jnp.concatenate([vt_s[:, pl.ds(0, keys)], vbt_s[...]], 1),
            jnp.concatenate([e_s[b, pl.ds(0, keys), :], pb_s[b]], 0),
        )
        if b == last:
            out = jnp.where(lane_live, out, 0.0)
        scatter(o_s, b, out.astype(bf16).T)
        yield
        dqt = nn(
            jnp.concatenate([kt_s[:, pl.ds(0, keys)], kbt_s[...]], 1),
            jnp.concatenate([sg_s[b, pl.ds(0, keys), :], sb_s[b]], 0),
        )
        scatter(dq_s, b, (dqt * SCALE).astype(bf16).T)
        yield
        used = pl.ds(0, keys)
        dk_s[used, :] += nn(sg_s[b, used, :], load(q_s, b))
        yield
        dv_s[used, :] += nn(e_s[b, used, :], load(g_s, b))

    def used_rest(members):
        return pl.ds(BMAX, (nb if last in members else seen) - BMAX)

    order = with_terms(beacon_rest, 2, used_rest)
    order += [own_part(0), own_part(1), own_part(2), call(lambda: send_terms(False))]
    interleave(order + [own_part(b) for b in range(3, last + 1)])

    dk_out[0:SPAN, :] = (dk_s[...] * SCALE).astype(bf16)
    dv_out[0:SPAN, :] = dv_s[...].astype(bf16)
    for step in range(1, n):
        @pl.when(me + step < n)
        def _():
            term_copy(step).wait_recv()
    total = term_s[mine, :]
    for step in range(1, n):
        total = total + recv_s[step - 1].astype(f32)
    dk_out[SPAN : SPAN + BMAX, :] = (total[:, 0:HD] * SCALE).astype(bf16)
    dv_out[SPAN : SPAN + BMAX, :] = total[:, HD : 2 * HD].astype(bf16)
    for step in range(1, n):
        @pl.when(me + step < n)
        def _():
            kv_copy(step).wait_send()
        @pl.when(me >= step)
        def _():
            term_copy(step).wait_send()


def write_kernel(o_s, dq_s, dk_s, dv_s, o_hbm, dq_hbm, dk_hbm, dv_hbm, sem):
    pairs = ((o_s, o_hbm), (dq_s, dq_hbm), (dk_s, dk_hbm), (dv_s, dv_hbm))
    copies = [
        pltpu.make_async_copy(src, dst, sem.at[i]) for i, (src, dst) in enumerate(pairs)
    ]
    for copy in copies:
        copy.start()
    for copy in copies:
        copy.wait()


def local(n, query_rows, key_rows, value_rows, out_grad, ratios):
    heads = query_rows.shape[1] // HD
    blocks = len(plan(heads)) + 1
    rows = query_rows.shape[0]
    bands = SPAN // SUB + 1
    nb = n * BMAX
    any_spec = pl.BlockSpec(memory_space=pltpu.HBM)
    vmem_spec = pl.BlockSpec(memory_space=pltpu.VMEM)
    dma = pltpu.SemaphoreType.DMA
    vmem = pltpu.VMEM
    args = [
        pltpu.with_memory_space_constraint(x, pltpu.HBM)
        for x in (ratios, query_rows, key_rows, value_rows, out_grad)
    ]
    parts = pl.pallas_call(
        functools.partial(kernel, n, heads),
        out_shape=(
            vmem(query_rows.shape, bf16),
            vmem(query_rows.shape, bf16),
            vmem(key_rows.shape, bf16),
            vmem(value_rows.shape, bf16),
        ),
        in_specs=[any_spec] * 5,
        out_specs=(vmem_spec,) * 4,
        scratch_shapes=[
            vmem(query_rows.shape, bf16),
            vmem(query_rows.shape, bf16),
            vmem((SPAN, HD), bf16),
            vmem((SPAN, HD), bf16),
            vmem((HD, SPAN), bf16),
            vmem((HD, SPAN), bf16),
            vmem((nb, 2 * HD), bf16),
            vmem((HD, nb), bf16),
            vmem((HD, nb), bf16),
            vmem((blocks, SPAN, BLK), f32),
            vmem((blocks, SPAN, BLK), f32),
            vmem((blocks, SPAN, BLK), bf16),
            vmem((blocks, SPAN, BLK), bf16),
            vmem((blocks, nb, BLK), bf16),
            vmem((blocks, nb, BLK), bf16),
            vmem((blocks, HD, BLK), bf16),
            vmem((blocks, HD, BLK), bf16),
            vmem((blocks, 8, BLK), f32),
            vmem((nb, BLK), f32),
            vmem((nb, BLK), f32),
            vmem((SUB, BLK), f32),
            vmem((BLK, BLK), f32),
            vmem((nb, 2 * HD), f32),
            vmem((nb, 2 * HD), bf16),
            vmem((n - 1, BMAX, 2 * HD), bf16),
            vmem((SPAN, HD), f32),
            vmem((SPAN, HD), f32),
            pltpu.SMEM((n,), jnp.int32), dma(()), dma((4,)), dma((bands,)), dma((bands,)),
            dma((n - 1,)), dma((n - 1,)), dma((n - 1,)), dma((n - 1,)),
        ],
        compiler_params=pltpu.CompilerParams(
            collective_id=0, has_side_effects=True, vmem_limit_bytes=60 << 20
        ),
        name="beacon_attention",
    )(*args)
    parts = [pltpu.with_memory_space_constraint(part, pltpu.VMEM) for part in parts]
    return pl.pallas_call(
        write_kernel,
        out_shape=(
            jax.ShapeDtypeStruct(query_rows.shape, bf16),
            jax.ShapeDtypeStruct(query_rows.shape, bf16),
            jax.ShapeDtypeStruct(key_rows.shape, bf16),
            jax.ShapeDtypeStruct(value_rows.shape, bf16),
        ),
        in_specs=[vmem_spec] * 4,
        out_specs=(any_spec,) * 4,
        scratch_shapes=[dma((4,))],
        name="write_rows",
    )(*parts)


def solution(mesh):
    rows = P(("seq", "span"), "kvg")
    return jax.shard_map(
        functools.partial(local, mesh.shape["span"]),
        mesh=mesh,
        in_specs=(rows, rows, rows, rows, P("seq")),
        out_specs=(rows, rows, rows, rows),
        check_vma=False,
    )
```
